512 devices in a mesh: expert: 8 (over x, core), replica: 64 (over y, z).
Axes of the slice: x: 4, y: 4, z: 16, core: 2. Of those that a mesh axis runs over, the one named last changes fastest.
Arguments:
- pool: bfloat16 [64, 4096, 2048], P('replica', 'expert'), may hold values from -15 to 15
- row_index: int32 [8, 64, 256], P(None, 'replica'), may hold values from 0 to 4095, as said below
- counts: int32 [8, 64], P('expert', 'replica'), may hold values from 128 to 256, as said below
- targets: bfloat16 [8, 64, 256, 384], P('expert', 'replica'), may hold values from -4 to 4
- weights: float32 [8, 2, 2048, 384], P('expert', None, 'replica'), may hold values from -0.125 to 0.125
- first_moment: float32 [8, 2, 2048, 384], P('expert', None, 'replica'), may hold values from -1.5 to 1.5
- second_moment: float32 [8, 2, 2048, 384], P('expert', None, 'replica'), may hold values from 0.0001 to 0.01
Outputs:
- new_weights: float32 [8, 2, 2048, 384], P('expert', None, 'replica')
- new_first_moment: float32 [8, 2, 2048, 384], P('expert', None, 'replica')
- new_second_moment: float32 [8, 2, 2048, 384], P('expert', None, 'replica')
The draws below stay inside these ranges and needn't reach their ends.
Inputs may be any that keep to these rules, and one draw needn't show every extreme that they name: `row_index`: for each expert and replica the 256 entries are distinct rows of that replica's 4096 tokens; at most 48 of them lie in any one aligned block of 512 rows, and some block holds exactly 48 of them. `counts`: at least 128 live slots for each expert on each replica; some expert on some replica has all 256 slots live.
All inputs are finite; a program needn't handle non-finite values.
Results may differ from the reference program's by a relative error of at most 0.0043.
Values may be sent and summed in bfloat16 or wider, within the bound.
A program may use at most 64 MiB of HBM per device.

```python
import math
import jax
import jax.numpy as jnp
from jax import lax

D = 2048
F = 384
TOKENS = 4096
STEP = 3
CAP = 256
EXPERTS = 8
REPLICAS = 64
SHARD_MOST = 48
LEVELS = 6


def draw_pool(key, part):
    block_rows = D // REPLICAS
    place = (jnp.arange(REPLICAS, dtype=jnp.float32) + jax.random.uniform(jax.random.fold_in(key, 41), (REPLICAS,), jnp.float32)) / REPLICAS
    block_mean = 2.0 * place
    column_scale = jnp.exp(jax.random.uniform(jax.random.fold_in(key, 43), (D,), jnp.float32, math.log(0.3), math.log(3.0)))
    noise = jax.random.truncated_normal(jax.random.fold_in(key, 44), -4.0, 4.0, (REPLICAS, TOKENS, D), jnp.float32)
    even_column = (jnp.arange(D, dtype=jnp.int32) % 2 == 0).astype(jnp.float32)
    column_mean = jnp.repeat(block_mean, block_rows) * even_column
    return (column_mean[None, None, :] + column_scale[None, None, :] * noise).astype(jnp.bfloat16)


def draw_row_index(key, part):
    shard_rows = TOKENS // EXPERTS
    base_share = CAP // EXPERTS
    extra_share = SHARD_MOST - base_share
    list_count = EXPERTS * REPLICAS
    pair_count = EXPERTS // 2
    shift_draw = jax.random.randint(jax.random.fold_in(key, 31), (list_count, pair_count), 0, extra_share + 1)
    forced_pair = jax.random.randint(jax.random.fold_in(key, 32), (list_count,), 0, pair_count)
    shifts = jnp.where(jnp.arange(pair_count, dtype=jnp.int32)[None, :] == forced_pair[:, None], extra_share, shift_draw)
    paired = jnp.stack([base_share + shifts, base_share - shifts], axis=2).reshape(list_count, EXPERTS)
    order_keys = jax.random.split(jax.random.fold_in(key, 33), list_count)
    shard_order = jax.vmap(lambda sub_key: jax.random.permutation(sub_key, EXPERTS))(order_keys)
    per_shard = jnp.take_along_axis(paired, shard_order, axis=1)
    row_keys = jax.random.split(jax.random.fold_in(key, 34), list_count * EXPERTS)
    picks = jax.vmap(lambda sub_key: jax.random.permutation(sub_key, shard_rows)[:SHARD_MOST])(row_keys)
    picks = picks.reshape(list_count, EXPERTS, SHARD_MOST)
    rows = picks + (jnp.arange(EXPERTS, dtype=jnp.int32) * shard_rows)[None, :, None]
    valid = (jnp.arange(SHARD_MOST, dtype=jnp.int32)[None, None, :] < per_shard[:, :, None]).astype(jnp.int32)
    total_candidates = EXPERTS * SHARD_MOST
    scores = (1 - valid.reshape(list_count, total_candidates)) * total_candidates + jnp.arange(total_candidates, dtype=jnp.int32)[None, :]
    chosen_order = jnp.argsort(scores, axis=1)[:, :CAP]
    chosen = jnp.take_along_axis(rows.reshape(list_count, total_candidates), chosen_order, axis=1)
    slot_keys = jax.random.split(jax.random.fold_in(key, 35), list_count)
    slot_order = jax.vmap(lambda sub_key: jax.random.permutation(sub_key, CAP))(slot_keys)
    result = jnp.take_along_axis(chosen, slot_order, axis=1)
    return result.reshape(EXPERTS, REPLICAS, CAP).astype(jnp.int32)


def draw_counts(key, part):
    drawn_counts = jax.random.randint(jax.random.fold_in(key, 21), (EXPERTS * REPLICAS,), CAP // 2, CAP + 1)
    full_place = jax.random.randint(jax.random.fold_in(key, 22), (), 0, EXPERTS * REPLICAS)
    places = jnp.arange(EXPERTS * REPLICAS, dtype=jnp.int32)
    filled = jnp.where(places == full_place, CAP, drawn_counts)
    return filled.reshape(EXPERTS, REPLICAS).astype(jnp.int32)


def draw_targets(key, part):
    signs = (2 * jax.random.randint(jax.random.fold_in(key, 51), (EXPERTS, 1, 1, F), 0, 2) - 1).astype(jnp.float32)
    level = jax.random.uniform(jax.random.fold_in(key, 52), (EXPERTS, 1, 1, F), jnp.float32, 0.5, 1.5)
    noise = 0.5 * jax.random.truncated_normal(jax.random.fold_in(key, 53), -4.0, 4.0, (EXPERTS, REPLICAS, CAP, F), jnp.float32)
    return (signs * level + noise).astype(jnp.bfloat16)


def block_levels(key, extent, cuts, smallest, largest):
    def one(dim, blocks):
        steps = jax.random.uniform(jax.random.fold_in(jax.random.fold_in(key, 6), dim), (blocks,), jnp.float32, smallest / len(cuts), largest / len(cuts))
        return jnp.repeat(jnp.exp(steps), extent[dim] // blocks).reshape((-1,) + (1,) * (len(extent) - dim - 1))

    factor_of = one(*cuts[0])
    for cut in cuts[1:]:
        factor_of = factor_of * one(*cut)
    return factor_of


def gaussian(stream_key, extent, scale, reach, cuts=(), held_as=jnp.bfloat16):
    values = jax.random.normal(stream_key, extent, jnp.float32) * scale
    if len(cuts) > 0:
        values = block_levels(stream_key, extent, cuts, -0.22, 0.18) * values
    return jnp.clip(values, min=-reach, max=reach).astype(held_as)


def setup_inputs(seed: int = 0) -> dict:
    key_of = jax.random.split(jax.random.key(seed), 8)
    pool = draw_pool(jax.random.fold_in(key_of[7], 71), 0)
    row_index = draw_row_index(jax.random.fold_in(key_of[7], 71), 0)
    counts = draw_counts(jax.random.fold_in(key_of[7], 71), 0)
    targets = draw_targets(jax.random.fold_in(key_of[7], 71), 0)
    weights = gaussian(key_of[4], (EXPERTS, 2, D, F), D ** -0.5, 0.125, ((0, 8), (2, 64)), jnp.float32)
    first_moment = gaussian(key_of[5], (EXPERTS, 2, D, F), 0.1, 1.5, ((0, 8), (2, 64)), jnp.float32)
    second_moment = jnp.clip(jnp.exp(math.log(0.01) - 4.6051702 * jax.random.uniform(key_of[6], (EXPERTS, 2, D, F), jnp.float32) ** block_levels(key_of[6], (EXPERTS, 2, D, F), ((0, 8), (2, 64)), -0.2, 0.2)), 0.0001, 0.01)
    return dict(pool=pool, row_index=row_index, counts=counts, targets=targets, weights=weights, first_moment=first_moment, second_moment=second_moment)


beta_first = 0.9
beta_second = 0.999
learning_rate = 0.02
decay_rate = 0.1
adam_epsilon = 1e-08
adasum_epsilon = 1e-12

def replica_gradient(pool_rows, selected, live_count, target_rows, gate_matrix, up_matrix):
    inputs = pool_rows[selected.astype(jnp.int32)]
    gate_value = jnp.dot(inputs, gate_matrix, preferred_element_type=jnp.float32)
    up_value = jnp.dot(inputs, up_matrix, preferred_element_type=jnp.float32)
    sigmoid = jax.nn.sigmoid(gate_value)
    activated = gate_value * sigmoid
    silu_slope = sigmoid * (1.0 + gate_value * (1.0 - sigmoid))
    live = (lax.iota(jnp.int32, selected.shape[0]) < live_count).astype(jnp.float32)[:, None]
    residual = (activated * up_value - target_rows.astype(jnp.float32)) * live / live_count.astype(jnp.float32)
    gate_delta = (residual * up_value * silu_slope).astype(jnp.bfloat16)
    up_delta = (residual * activated).astype(jnp.bfloat16)
    gate_grad = jnp.dot(inputs.T, gate_delta, preferred_element_type=jnp.float32)
    up_grad = jnp.dot(inputs.T, up_delta, preferred_element_type=jnp.float32)
    return jnp.stack([gate_grad, up_grad])

def adasum_tree(gradients):
    for level_number in range(LEVELS):
        half_count = gradients.shape[0] // 2
        first_group = gradients[:half_count]
        second_group = gradients[half_count:]
        inner_product = lax.optimization_barrier(jnp.sum(first_group * second_group, axis=(2, 3), keepdims=True))
        first_square = lax.optimization_barrier(jnp.sum(first_group * first_group, axis=(2, 3), keepdims=True))
        second_square = lax.optimization_barrier(jnp.sum(second_group * second_group, axis=(2, 3), keepdims=True))
        first_weight = 1.0 - inner_product / (2.0 * first_square + adasum_epsilon)
        second_weight = 1.0 - inner_product / (2.0 * second_square + adasum_epsilon)
        gradients = first_weight * first_group + second_weight * second_group
    return gradients[0]

def adam_update(gradient, weight, moment_one, moment_two):
    moment_one = beta_first * moment_one + (1.0 - beta_first) * gradient
    moment_two = beta_second * moment_two + (1.0 - beta_second) * gradient * gradient
    first_hat = moment_one / (1.0 - beta_first ** STEP)
    second_hat = moment_two / (1.0 - beta_second ** STEP)
    weight = weight - learning_rate * (first_hat / (jnp.sqrt(second_hat) + adam_epsilon) + decay_rate * weight)
    return (weight, moment_one, moment_two)

def reference(pool, row_index, counts, targets, weights, first_moment, second_moment):
    lowered = weights.astype(jnp.bfloat16)

    def one_expert(expert_args):
        expert_rows, expert_counts, expert_targets, expert_lowered, expert_weight, moment_one, moment_two = expert_args

        def one_replica(replica_args):
            pool_rows, selected, live_count, target_rows = replica_args
            return replica_gradient(pool_rows, selected, live_count, target_rows, expert_lowered[0], expert_lowered[1])
        gradients = lax.map(one_replica, (pool, expert_rows, expert_counts, expert_targets))
        combined = adasum_tree(gradients)
        return adam_update(combined, expert_weight, moment_one, moment_two)
    return lax.map(one_expert, (row_index, counts, targets, lowered, weights, first_moment, second_moment))
```

```python
import functools

import jax
import jax.numpy as jnp
from jax import lax
from jax.experimental import pallas as pl
from jax.experimental.pallas import tpu as pltpu
from jax.sharding import PartitionSpec as P

STEP = 3
MESH = pl.DeviceIdType.MESH
NE, NY, NZ = 8, 4, 16
NR = NY * NZ
CAP = 256
HELD = 48
D = 2048
F = 384
SHARD = 512
Q = D // NY
ROWS = D // NR
LIST = NE * HELD

beta_first = 0.9
beta_second = 0.999
learning_rate = 0.02
decay_rate = 0.1
adam_epsilon = 1e-08
adasum_epsilon = 1e-12

f32 = jnp.float32
bf16 = jnp.bfloat16
i32 = jnp.int32

X_OFFSETS = (4, 3, 5, 2, 6, 7, 1)
Y_OFFSETS = (2, 1, 3)
Z_OFFSETS = (8, 7, 9, 6, 10, 5, 11, 4, 12, 3, 13, 2, 14, 1, 15)


def iota(shape, dim):
    return lax.broadcasted_iota(i32, shape, dim)


def adam_update(gradient, weight, moment_one, moment_two):
    moment_one = beta_first * moment_one + (1.0 - beta_first) * gradient
    moment_two = beta_second * moment_two + (1.0 - beta_second) * gradient * gradient
    first_hat = moment_one / (1.0 - beta_first**STEP)
    second_hat = moment_two / (1.0 - beta_second**STEP)
    weight = weight - learning_rate * (
        first_hat / (jnp.sqrt(second_hat) + adam_epsilon) + decay_rate * weight
    )
    return (weight, moment_one, moment_two)


def pair_weights(inner, first_square, second_square):
    first = 1.0 - inner / (2.0 * first_square + adasum_epsilon)
    second = 1.0 - inner / (2.0 * second_square + adasum_epsilon)
    return first, second


def four_coefficients(rows):
    g = lambda a, b: rows[4 * a + b : 4 * a + b + 1, :]
    w0, w2 = pair_weights(g(0, 2), g(0, 0), g(2, 2))
    w1, w3 = pair_weights(g(1, 3), g(1, 1), g(3, 3))
    qa = w0 * w0 * g(0, 0) + 2.0 * w0 * w2 * g(0, 2) + w2 * w2 * g(2, 2)
    qb = w1 * w1 * g(1, 1) + 2.0 * w1 * w3 * g(1, 3) + w3 * w3 * g(3, 3)
    qa = jnp.maximum(qa, 0.0)
    qb = jnp.maximum(qb, 0.0)
    pab = w0 * (w1 * g(0, 1) + w3 * g(0, 3)) + w2 * (w1 * g(2, 1) + w3 * g(2, 3))
    va, vb = pair_weights(pab, qa, qb)
    return (va * w0, vb * w1, va * w2, vb * w3)


def ring_coefficients(gram):
    row = iota((NZ, 128), 0)
    lane = iota((NZ, 128), 1)
    coefficient = jnp.ones((NZ, 1), f32)
    for half in (8, 4, 2, 1):
        zero = jnp.zeros_like(gram)
        p_col = jnp.sum(jnp.where(lane == (row + half) % NZ, gram, zero), axis=1, keepdims=True)
        q_col = jnp.sum(jnp.where(lane == row, gram, zero), axis=1, keepdims=True)
        p_row = jnp.sum(
            jnp.where(row == (lane + half) % NZ, gram, zero), axis=0, keepdims=True
        )
        q_row = jnp.sum(jnp.where(row == lane % NZ, gram, zero), axis=0, keepdims=True)
        w_col = 1.0 - p_col / (2.0 * jnp.maximum(q_col, 0.0) + adasum_epsilon)
        w_row = 1.0 - p_row / (2.0 * jnp.maximum(q_row, 0.0) + adasum_epsilon)
        scaled = w_col * gram * w_row
        folded = scaled + pltpu.roll(scaled, half, 1)
        gram = folded + pltpu.roll(folded, half, 0)
        coefficient = coefficient * w_col
    return coefficient


def lanes(row):
    return jnp.concatenate([row] * (F // 128), axis=1)


def wait_bytes(ref, sem):
    pltpu.make_async_copy(ref, ref, sem).wait()


def step_kernel(
    rows_ref,
    count_ref,
    pool_hbm,
    targets_hbm,
    weights_ref,
    out_ref,
    pool_v,
    targets_v,
    held_v,
    pick_v,
    place_v,
    sent_rows,
    got_rows,
    x_v,
    x_got,
    x_turned,
    gate_w,
    up_w,
    act_v,
    deltas,
    grads,
    gram_y,
    item_out,
    item_in,
    tab_y,
    tab_z,
    load_sem,
    send_sem,
    rows_sem,
    gy_sem,
    gp_sem,
    gm_sem,
    up_sem,
    um_sem,
    uy_sem,
    x_sem,
    delta_sem,
    gram_sem,
    item_sem,
    ty_sem,
    tz_sem,
):
    me = lax.axis_index("expert")
    rep = lax.axis_index("replica")
    y = rep // NZ
    z = rep % NZ

    def at_e(off):
        return ((me + off) % NE, rep)

    def at_y(off):
        return (me, ((y + off) % NY) * NZ + z)

    def at_z(off):
        return (me, y * NZ + (z + off) % NZ)

    def send(src, dst, group, recv, device):
        pltpu.make_async_remote_copy(
            src_ref=src,
            dst_ref=dst,
            send_sem=send_sem.at[group],
            recv_sem=recv,
            device_id=device,
            device_id_type=MESH,
        ).start()

    barrier = pltpu.get_barrier_semaphore()
    peers = [at_e(o) for o in X_OFFSETS] + [at_y(o) for o in Y_OFFSETS] + [at_z(1), at_z(NZ - 1)]
    for device in peers:
        pl.semaphore_signal(barrier, inc=1, device_id=device, device_id_type=MESH)

    loads = [
        pltpu.make_async_copy(
            pool_hbm.at[0, :, pl.ds(q * Q, Q)], pool_v.at[q], load_sem.at[q]
        )
        for q in range(NY)
    ]
    loads.append(pltpu.make_async_copy(targets_hbm.at[0, 0], targets_v, load_sem.at[NY]))
    for load in loads:
        load.start()

    gate_w[rep] = weights_ref[0, 0].astype(bf16)
    up_w[rep] = weights_ref[0, 1].astype(bf16)

    pl.semaphore_wait(barrier, len(peers))

    for k, off in enumerate(Y_OFFSETS):
        send(gate_w.at[rep], gate_w.at[rep], 0, gy_sem.at[off - 1], at_y(off))
    send(up_w.at[rep], up_w.at[rep], 1, up_sem.at[0], at_z(1))
    send(up_w.at[rep], up_w.at[rep], 1, um_sem.at[0], at_z(NZ - 1))
    send(gate_w.at[rep], gate_w.at[rep], 0, gp_sem.at[0, 0], at_z(1))
    send(gate_w.at[rep], gate_w.at[rep], 0, gm_sem.at[0, 0], at_z(NZ - 1))
    for off in Y_OFFSETS:
        send(up_w.at[rep], up_w.at[rep], 1, uy_sem.at[0, off - 1], at_y(off))

    for e in range(NE):
        listed = rows_ref[e]
        held_v[e : e + 1, :] = jnp.where(listed // SHARD == me, 1.0, 0.0)
    before = jnp.where(iota((CAP, CAP), 0) < iota((CAP, CAP), 1), 1.0, 0.0).astype(bf16)
    held = held_v[...]
    rank = jnp.dot(held.astype(bf16), before, preferred_element_type=f32)
    held_v[...] = jnp.where(held > 0.5, rank, -1.0)
    for e in range(NE):
        key = jnp.broadcast_to(held_v[e : e + 1, :], (HELD, CAP))
        local = jnp.broadcast_to((rows_ref[e] - me * SHARD + 1).astype(f32), (HELD, CAP))
        match = key == iota((HELD, CAP), 0).astype(f32)
        index = jnp.sum(jnp.where(match, local, 0.0), axis=1, keepdims=True) - 1.0
        pick_v[pl.ds(e * HELD, HELD), :] = jnp.where(
            index == iota((HELD, SHARD), 1).astype(f32), 1.0, 0.0
        ).astype(bf16)

    def gather(i):
        q = (y + (Y_OFFSETS + (0,))[i]) % NY
        found = jnp.dot(pick_v[...], pool_v[q], preferred_element_type=f32).astype(bf16)
        sent_rows[pl.ds(q * NE, NE)] = found.reshape(NE, HELD, Q)
        for j, off in enumerate(X_OFFSETS):
            send(
                sent_rows.at[q * NE + (me + off) % NE],
                got_rows.at[q * NE + me],
                2,
                rows_sem.at[i, j],
                at_e(off),
            )
        got_rows[q * NE + me] = sent_rows[q * NE + me]

    for load in loads:
        load.wait()
    gather(0)

    for off in Y_OFFSETS:
        row = ((y + NY - off) % NY) * NZ + z
        pltpu.make_async_copy(gate_w.at[row], gate_w.at[row], gy_sem.at[off - 1]).wait()
        send(gate_w.at[row], gate_w.at[row], 0, gp_sem.at[0, off], at_z(1))
        send(gate_w.at[row], gate_w.at[row], 0, gm_sem.at[0, off], at_z(NZ - 1))

    gather(1)
    gather(2)
    gather(3)

    own_row = rows_ref[me].astype(f32)
    square = jnp.broadcast_to(own_row, (CAP, CAP))
    sub = iota((CAP, CAP), 0)
    lan = iota((CAP, CAP), 1)
    own_col = jnp.sum(jnp.where(sub == lan, square, 0.0), axis=1, keepdims=True)
    shard_row = rows_ref[me] // SHARD
    shard_col = own_col.astype(i32) // SHARD
    same = jnp.logical_and(jnp.broadcast_to(shard_row, (CAP, CAP)) == shard_col, lan < sub)
    rank_col = jnp.sum(jnp.where(same, 1.0, 0.0), axis=1, keepdims=True)
    place = shard_col * HELD + rank_col.astype(i32)
    place_v[...] = jnp.where(place == iota((CAP, LIST), 1), 1.0, 0.0).astype(bf16)

    def gate_wait(sem, k, off, back):
        row = ((y + NY - off) % NY) * NZ + (z + NZ - k * back) % NZ
        pltpu.make_async_copy(gate_w.at[row], gate_w.at[row], sem.at[k - 1, off]).wait()
        return row

    def up_wait(sem, k, back):
        row = y * NZ + (z + NZ - k * back) % NZ
        pltpu.make_async_copy(up_w.at[row], up_w.at[row], sem.at[k - 1]).wait()
        return row

    def up_across(row, slot):
        for off in Y_OFFSETS:
            send(up_w.at[row], up_w.at[row], 1, uy_sem.at[slot, off - 1], at_y(off))

    def ring(k, plus, minus):
        row = up_wait(up_sem, k, 1)
        if plus:
            send(up_w.at[row], up_w.at[row], 1, up_sem.at[k], at_z(1))
        up_across(row, k)
        if minus is not None:
            row = up_wait(um_sem, k, NZ - 1)
            if minus:
                send(up_w.at[row], up_w.at[row], 1, um_sem.at[k], at_z(NZ - 1))
            up_across(row, k + 8)
        for off in (0,) + Y_OFFSETS:
            row = gate_wait(gp_sem, k, off, 1)
            if plus:
                send(gate_w.at[row], gate_w.at[row], 0, gp_sem.at[k, off], at_z(1))
            if minus is not None:
                row = gate_wait(gm_sem, k, off, NZ - 1)
                if minus:
                    send(gate_w.at[row], gate_w.at[row], 0, gm_sem.at[k, off], at_z(NZ - 1))

    @pl.loop(1, 7)
    def _(k):
        ring(k, True, True)

    ring(7, True, False)
    ring(8, False, None)

    for i, y_off in enumerate(Y_OFFSETS + (0,)):
        q = (y + y_off) % NY
        for j, off in enumerate(X_OFFSETS):
            slot = q * NE + (me + NE - off) % NE
            pltpu.make_async_copy(
                got_rows.at[slot], got_rows.at[slot], rows_sem.at[i, j]
            ).wait()
        block = got_rows[pl.ds(q * NE, NE)].reshape(LIST, Q)
        ordered = jnp.dot(place_v[...], block, preferred_element_type=f32).astype(bf16)
        x_v[q] = ordered
        if y_off:
            send(x_v.at[q], x_got.at[y], 3, x_sem.at[y_off - 1], at_y(y_off))
        else:
            x_got[y] = ordered

    @pl.loop(0, NZ)
    def _(slot):
        back = jnp.where(slot < 9, NZ - slot, slot - 8)
        for off in Y_OFFSETS:
            row = ((y + NY - off) % NY) * NZ + (z + back) % NZ
            pltpu.make_async_copy(up_w.at[row], up_w.at[row], uy_sem.at[slot, off - 1]).wait()

    for m, w in enumerate((gate_w, up_w)):
        total = None
        for q in range(NY):
            part = jnp.dot(
                x_v[q], w[pl.ds(q * NZ, NZ)].reshape(Q, F), preferred_element_type=f32
            )
            total = part if total is None else total + part
        act_v[m] = total

    count = count_ref[...]

    @pl.loop(0, CAP // 32)
    def _(i):
        span = pl.ds(pl.multiple_of(i * 32, 32), 32)
        gate_value = act_v[0, span, :]
        up_value = act_v[1, span, :]
        sigmoid = 1.0 / (1.0 + jnp.exp(-gate_value))
        activated = gate_value * sigmoid
        slope = sigmoid * (1.0 + gate_value * (1.0 - sigmoid))
        live = jnp.where(iota((32, F), 0) + i * 32 < count, 1.0, 0.0)
        residual = (
            (activated * up_value - targets_v[span, :].astype(f32)) * live / count.astype(f32)
        )
        deltas[y, span, :] = (residual * up_value * slope).astype(bf16)
        deltas[NY + y, span, :] = (residual * activated).astype(bf16)

    for m in range(2):
        for off in Y_OFFSETS:
            send(
                deltas.at[m * NY + y],
                deltas.at[m * NY + y],
                4,
                delta_sem.at[m, off - 1],
                at_y(off),
            )

    for off in Y_OFFSETS:
        src = (y + NY - off) % NY
        pltpu.make_async_copy(x_got.at[src], x_got.at[src], x_sem.at[off - 1]).wait()
    for s in range(NY):
        x_turned[s] = x_got[s].T

    for m in range(2):
        for off in Y_OFFSETS:
            src = m * NY + (y + NY - off) % NY
            pltpu.make_async_copy(
                deltas.at[src], deltas.at[src], delta_sem.at[m, off - 1]
            ).wait()
        for s in range(NY):
            grads[m * NY + s] = jnp.dot(
                x_turned[s], deltas[m * NY + s], preferred_element_type=f32
            )
        pairs = [(a, b) for a in range(NY) for b in range(a, NY)]

        def add_products(i, sums):
            span = pl.ds(pl.multiple_of(i * 8, 8), 8)
            parts = [grads[m * NY + s, span, :] for s in range(NY)]
            out = []
            for (a, b), old in zip(pairs, sums):
                product = parts[a] * parts[b]
                for c in range(F // 128):
                    old = old + product[:, c * 128 : c * 128 + 128]
                out.append(old)
            return tuple(out)

        sums = lax.fori_loop(
            0, Q // 8, add_products, tuple(jnp.zeros((8, 128), f32) for _ in pairs)
        )
        for (a, b), value in zip(pairs, sums):
            line = jnp.sum(value, axis=0, keepdims=True)
            gram_y[m * NY + y, 4 * a + b : 4 * a + b + 1, :] = line
            if a != b:
                gram_y[m * NY + y, 4 * b + a : 4 * b + a + 1, :] = line
        for off in Y_OFFSETS:
            send(
                gram_y.at[m * NY + y],
                gram_y.at[m * NY + y],
                5,
                gram_sem.at[m, off - 1],
                at_y(off),
            )

    for m in range(2):
        for off in Y_OFFSETS:
            src = m * NY + (y + NY - off) % NY
            pltpu.make_async_copy(
                gram_y.at[src], gram_y.at[src], gram_sem.at[m, off - 1]
            ).wait()
        table = gram_y[m * NY]
        for s in range(1, NY):
            table = table + gram_y[m * NY + s]
        table = jnp.broadcast_to(jnp.sum(table, axis=1, keepdims=True), (16, 128))
        scale = [lanes(c) for c in four_coefficients(table)]
        for off in Z_OFFSETS + (0,):
            to = (z + off) % NZ
            span = pl.ds(pl.multiple_of(to * ROWS, ROWS), ROWS)
            item = scale[0] * grads[m * NY, span, :]
            for s in range(1, NY):
                item = item + scale[s] * grads[m * NY + s, span, :]
            if off:
                item_out[m * NZ + to] = item.astype(bf16)
                send(
                    item_out.at[m * NZ + to],
                    item_in.at[m * NZ + z],
                    6,
                    item_sem.at[m, off - 1],
                    at_z(off),
                )
            else:
                item_in[m * NZ + z] = item.astype(bf16)

    block = NZ * ROWS
    grams = []
    for m in range(2):
        for off in Z_OFFSETS:
            src = m * NZ + (z + NZ - off) % NZ
            pltpu.make_async_copy(
                item_in.at[src], item_in.at[src], item_sem.at[m, off - 1]
            ).wait()
        items = item_in[pl.ds(m * NZ, NZ)].reshape(block, F)
        product = lax.dot_general(
            items, items, (((1,), (1,)), ((), ())), preferred_element_type=f32
        )
        product = jnp.where(
            iota((block, block), 0) % ROWS == iota((block, block), 1) % ROWS, product, 0.0
        )
        product = jnp.sum(product.reshape(NZ, ROWS, block), axis=1)
        fold = jnp.where(
            iota((block, 128), 0) // ROWS == iota((block, 128), 1) % NZ, 1.0, 0.0
        )
        grams.append(
            jnp.dot(
                product, fold, precision=lax.Precision.HIGHEST, preferred_element_type=f32
            )
        )
    part = iota((8, 128), 1) // 32
    packed = jnp.where(part == 0, grams[0][0:8], 0.0)
    packed = jnp.where(part == 1, grams[0][8:16], packed)
    packed = jnp.where(part == 2, grams[1][0:8], packed)
    packed = jnp.where(part == 3, grams[1][8:16], packed)
    tab_y[y] = packed
    for off in Y_OFFSETS:
        send(tab_y.at[y], tab_y.at[y], 7, ty_sem.at[off - 1], at_y(off))
    for off in Y_OFFSETS:
        src = (y + NY - off) % NY
        pltpu.make_async_copy(tab_y.at[src], tab_y.at[src], ty_sem.at[off - 1]).wait()
    packed = tab_y[0]
    for s in range(1, NY):
        packed = packed + tab_y[s]
    tab_z[z] = packed
    for off in Z_OFFSETS:
        send(tab_z.at[z], tab_z.at[z], 8, tz_sem.at[off - 1], at_z(off))
    for off in Z_OFFSETS:
        src = (z + NZ - off) % NZ
        pltpu.make_async_copy(tab_z.at[src], tab_z.at[src], tz_sem.at[off - 1]).wait()
    packed = tab_z[0]
    for s in range(1, NZ):
        packed = packed + tab_z[s]

    def spread(which):
        one = jnp.where(part == which, packed, 0.0)
        one = one + pltpu.roll(one, 32, 1)
        return one + pltpu.roll(one, 64, 1)

    for m in range(2):
        gram = jnp.concatenate([spread(2 * m), spread(2 * m + 1)], axis=0)
        scale = jnp.broadcast_to(ring_coefficients(gram), (NZ, 128))
        total = None
        for s in range(NZ):
            term = lanes(scale[s : s + 1, :]) * item_in[m * NZ + s].astype(f32)
            total = term if total is None else total + term
        out_ref[m] = total

    wait_bytes(gate_w.at[pl.ds(0, 63)], send_sem.at[0])
    wait_bytes(up_w.at[pl.ds(0, 63)], send_sem.at[1])
    wait_bytes(sent_rows.at[pl.ds(0, 28)], send_sem.at[2])
    wait_bytes(x_v.at[pl.ds(0, 3)], send_sem.at[3])
    wait_bytes(deltas.at[pl.ds(0, 6)], send_sem.at[4])
    wait_bytes(gram_y.at[pl.ds(0, 6)], send_sem.at[5])
    wait_bytes(item_out.at[pl.ds(0, 30)], send_sem.at[6])
    wait_bytes(tab_y.at[pl.ds(0, 3)], send_sem.at[7])
    wait_bytes(tab_z.at[pl.ds(0, 15)], send_sem.at[8])


def combined_gradient(pool, row_index, counts, targets, weights):
    vmem = pl.BlockSpec(memory_space=pltpu.VMEM)
    anywhere = pl.BlockSpec(memory_space=pl.ANY)
    dma = pltpu.SemaphoreType.DMA
    return pl.pallas_call(
        step_kernel,
        out_shape=jax.ShapeDtypeStruct((2, ROWS, F), f32),
        in_specs=[vmem, vmem, anywhere, anywhere, vmem],
        out_specs=vmem,
        scratch_shapes=[
            pltpu.VMEM((NY, SHARD, Q), bf16),
            pltpu.VMEM((CAP, F), bf16),
            pltpu.VMEM((NE, CAP), f32),
            pltpu.VMEM((LIST, SHARD), bf16),
            pltpu.VMEM((CAP, LIST), bf16),
            pltpu.VMEM((NY * NE, HELD, Q), bf16),
            pltpu.VMEM((NY * NE, HELD, Q), bf16),
            pltpu.VMEM((NY, CAP, Q), bf16),
            pltpu.VMEM((NY, CAP, Q), bf16),
            pltpu.VMEM((NY, Q, CAP), bf16),
            pltpu.VMEM((NR, ROWS, F), bf16),
            pltpu.VMEM((NR, ROWS, F), bf16),
            pltpu.VMEM((2, CAP, F), f32),
            pltpu.VMEM((2 * NY, CAP, F), bf16),
            pltpu.VMEM((2 * NY, Q, F), f32),
            pltpu.VMEM((2 * NY, 16, 128), f32),
            pltpu.VMEM((2 * NZ, ROWS, F), bf16),
            pltpu.VMEM((2 * NZ, ROWS, F), bf16),
            pltpu.VMEM((NY, 8, 128), f32),
            pltpu.VMEM((NZ, 8, 128), f32),
            dma((NY + 1,)),
            dma((9,)),
            dma((NY, NE - 1)),
            dma((NY - 1,)),
            dma((8, NY)),
            dma((7, NY)),
            dma((8,)),
            dma((7,)),
            dma((NZ, NY - 1)),
            dma((NY - 1,)),
            dma((2, NY - 1)),
            dma((2, NY - 1)),
            dma((2, NZ - 1)),
            dma((NY - 1,)),
            dma((NZ - 1,)),
        ],
        compiler_params=pltpu.CompilerParams(
            collective_id=0, has_side_effects=True, vmem_limit_bytes=56 * 1024 * 1024
        ),
    )(row_index, counts, pool, targets, weights)


def shards(pool, row_index, counts, targets, weights, first_moment, second_moment):
    combined = combined_gradient(pool, row_index, counts, targets, weights)
    new_weight, moment_one, moment_two = adam_update(
        combined, weights[0], first_moment[0], second_moment[0]
    )
    return (new_weight[None], moment_one[None], moment_two[None])


def solution(mesh):
    in_specs = (
        P("replica", "expert", None),
        P(None, "replica", None),
        P("expert", "replica"),
        P("expert", "replica", None, None),
        P("expert", None, "replica", None),
        P("expert", None, "replica", None),
        P("expert", None, "replica", None),
    )
    out_specs = (P("expert", None, "replica", None),) * 3
    return jax.shard_map(
        shards, mesh=mesh, in_specs=in_specs, out_specs=out_specs, check_vma=False
    )
```

```python
import functools

import jax
import jax.numpy as jnp
from jax import lax
from jax.experimental import pallas as pl
from jax.experimental.pallas import tpu as pltpu
from jax.sharding import PartitionSpec as P

STEP = 3
MESH = pl.DeviceIdType.MESH
NE, NY, NZ = 8, 4, 16
NR = NY * NZ
CAP = 256
HELD = 48
D = 2048
F = 384
SHARD = 512
Q = D // NY
ROWS = D // NR
LIST = NE * HELD
HALF = CAP // 2
BOTH = 2 * F
FIRST = 512

beta_first = 0.9
beta_second = 0.999
learning_rate = 0.02
decay_rate = 0.1
adam_epsilon = 1e-08
adasum_epsilon = 1e-12

f32 = jnp.float32
bf16 = jnp.bfloat16
i32 = jnp.int32

X_OFFSETS = (4, 3, 5, 2, 6, 7, 1)
Y_OFFSETS = (2, 1, 3)
Z_OFFSETS = (8, 7, 9, 6, 10, 5, 11, 4, 12, 3, 13, 2, 14, 1, 15)


def iota(shape, dim):
    return lax.broadcasted_iota(i32, shape, dim)


def adam_update(gradient, weight, moment_one, moment_two):
    moment_one = beta_first * moment_one + (1.0 - beta_first) * gradient
    moment_two = beta_second * moment_two + (1.0 - beta_second) * gradient * gradient
    first_hat = moment_one / (1.0 - beta_first**STEP)
    second_hat = moment_two / (1.0 - beta_second**STEP)
    weight = weight - learning_rate * (
        first_hat / (jnp.sqrt(second_hat) + adam_epsilon) + decay_rate * weight
    )
    return (weight, moment_one, moment_two)


def pair_weights(inner, first_square, second_square):
    first = 1.0 - inner / (2.0 * first_square + adasum_epsilon)
    second = 1.0 - inner / (2.0 * second_square + adasum_epsilon)
    return first, second


def four_coefficients(rows):
    g = lambda a, b: rows[4 * a + b : 4 * a + b + 1, :]
    w0, w2 = pair_weights(g(0, 2), g(0, 0), g(2, 2))
    w1, w3 = pair_weights(g(1, 3), g(1, 1), g(3, 3))
    qa = w0 * w0 * g(0, 0) + 2.0 * w0 * w2 * g(0, 2) + w2 * w2 * g(2, 2)
    qb = w1 * w1 * g(1, 1) + 2.0 * w1 * w3 * g(1, 3) + w3 * w3 * g(3, 3)
    qa = jnp.maximum(qa, 0.0)
    qb = jnp.maximum(qb, 0.0)
    pab = w0 * (w1 * g(0, 1) + w3 * g(0, 3)) + w2 * (w1 * g(2, 1) + w3 * g(2, 3))
    va, vb = pair_weights(pab, qa, qb)
    return (va * w0, vb * w1, va * w2, vb * w3)


def ring_coefficients(gram):
    row = iota((NZ, 128), 0)
    lane = iota((NZ, 128), 1)
    coefficient = jnp.ones((NZ, 1), f32)
    for half in (8, 4, 2, 1):
        zero = jnp.zeros_like(gram)
        p_col = jnp.sum(jnp.where(lane == (row + half) % NZ, gram, zero), axis=1, keepdims=True)
        q_col = jnp.sum(jnp.where(lane == row, gram, zero), axis=1, keepdims=True)
        p_row = jnp.sum(
            jnp.where(row == (lane + half) % NZ, gram, zero), axis=0, keepdims=True
        )
        q_row = jnp.sum(jnp.where(row == lane % NZ, gram, zero), axis=0, keepdims=True)
        w_col = 1.0 - p_col / (2.0 * jnp.maximum(q_col, 0.0) + adasum_epsilon)
        w_row = 1.0 - p_row / (2.0 * jnp.maximum(q_row, 0.0) + adasum_epsilon)
        scaled = w_col * gram * w_row
        folded = scaled + pltpu.roll(scaled, half, 1)
        gram = folded + pltpu.roll(folded, half, 0)
        coefficient = coefficient * w_col
    return coefficient


def lanes(row):
    return jnp.concatenate([row] * (F // 128), axis=1)


def step_kernel(
    rows_ref,
    count_ref,
    pool_hbm,
    targets_hbm,
    weights_ref,
    out_ref,
    pool_v,
    targets_v,
    held_v,
    pick_v,
    place_v,
    sent_rows,
    got_rows,
    x_v,
    x_got,
    x_turned,
    gate_w,
    up_w,
    act_v,
    deltas,
    grads,
    gram_y,
    item_out,
    item_in,
    tab_y,
    tab_z,
    load_sem,
    send_sem,
    rows_sem,
    gy_sem,
    gp_sem,
    gm_sem,
    up_sem,
    um_sem,
    uy_sem,
    x_sem,
    delta_sem,
    gram_sem,
    item_sem,
    ty_sem,
    tz_sem,
):
    me = lax.axis_index("expert")
    rep = lax.axis_index("replica")
    y = rep // NZ
    z = rep % NZ

    def at_e(off):
        return ((me + off) % NE, rep)

    def at_y(off):
        return (me, ((y + off) % NY) * NZ + z)

    def at_z(off):
        return (me, y * NZ + (z + off) % NZ)

    def send(src, dst, group, recv, device):
        pltpu.make_async_remote_copy(
            src_ref=src,
            dst_ref=dst,
            send_sem=send_sem.at[group],
            recv_sem=recv,
            device_id=device,
            device_id_type=MESH,
        ).start()

    def arrive(ref, sem, group):
        pltpu.make_async_copy(ref, ref, sem).wait()

    barrier = pltpu.get_barrier_semaphore()
    peers = [at_e(o) for o in X_OFFSETS] + [at_y(o) for o in Y_OFFSETS] + [at_z(1), at_z(NZ - 1)]
    for device in peers:
        pl.semaphore_signal(barrier, inc=1, device_id=device, device_id_type=MESH)

    loads = [
        pltpu.make_async_copy(
            pool_hbm.at[0, :, pl.ds(q * Q, Q)], pool_v.at[q], load_sem.at[q]
        )
        for q in range(NY)
    ]
    loads.append(pltpu.make_async_copy(targets_hbm.at[0, 0], targets_v, load_sem.at[NY]))
    for load in loads:
        load.start()

    gate_w[rep, :, pl.ds(0, F)] = weights_ref[0, 0].astype(bf16)
    gate_w[rep, :, pl.ds(F, FIRST - F)] = weights_ref[0, 1, :, pl.ds(0, FIRST - F)].astype(bf16)
    up_w[rep] = weights_ref[0, 1, :, pl.ds(FIRST - F, BOTH - FIRST)].astype(bf16)

    for e in range(NE):
        listed = rows_ref[e]
        held_v[e : e + 1, :] = jnp.where(listed // SHARD == me, 1.0, 0.0)
    before = jnp.where(iota((CAP, CAP), 0) < iota((CAP, CAP), 1), 1.0, 0.0).astype(bf16)
    held = held_v[...]
    rank = jnp.dot(held.astype(bf16), before, preferred_element_type=f32)
    held_v[...] = jnp.where(held > 0.5, rank, -1.0)
    for e in range(NE):
        key = jnp.broadcast_to(held_v[e : e + 1, :], (HELD, CAP))
        local = jnp.broadcast_to((rows_ref[e] - me * SHARD + 1).astype(f32), (HELD, CAP))
        match = key == iota((HELD, CAP), 0).astype(f32)
        index = jnp.sum(jnp.where(match, local, 0.0), axis=1, keepdims=True) - 1.0
        pick_v[pl.ds(e * HELD, HELD), :] = jnp.where(
            index == iota((HELD, SHARD), 1).astype(f32), 1.0, 0.0
        ).astype(bf16)

    pl.semaphore_wait(barrier, len(peers))

    for off in Y_OFFSETS:
        send(gate_w.at[rep], gate_w.at[rep], 0, gy_sem.at[off - 1], at_y(off))
    send(up_w.at[rep], up_w.at[rep], 1, up_sem.at[0], at_z(1))
    send(up_w.at[rep], up_w.at[rep], 1, um_sem.at[0], at_z(NZ - 1))
    send(gate_w.at[rep], gate_w.at[rep], 0, gp_sem.at[0, 0], at_z(1))
    send(gate_w.at[rep], gate_w.at[rep], 0, gm_sem.at[0, 0], at_z(NZ - 1))
    for off in Y_OFFSETS:
        send(up_w.at[rep], up_w.at[rep], 1, uy_sem.at[0, off - 1], at_y(off))

    def gather(i):
        q = (y + (Y_OFFSETS + (0,))[i]) % NY
        found = jnp.dot(pick_v[...], pool_v[q], preferred_element_type=f32).astype(bf16)
        sent_rows[pl.ds(q * NE, NE)] = found.reshape(NE, HELD, Q)
        for j, off in enumerate(X_OFFSETS):
            send(
                sent_rows.at[q * NE + (me + off) % NE],
                got_rows.at[q * NE + me],
                2,
                rows_sem.at[i, j],
                at_e(off),
            )
        got_rows[q * NE + me] = sent_rows[q * NE + me]

    def own_places():
        own_row = rows_ref[me].astype(f32)
        square = jnp.broadcast_to(own_row, (CAP, CAP))
        sub = iota((CAP, CAP), 0)
        lan = iota((CAP, CAP), 1)
        own_col = jnp.sum(jnp.where(sub == lan, square, 0.0), axis=1, keepdims=True)
        shard_row = rows_ref[me] // SHARD
        shard_col = own_col.astype(i32) // SHARD
        same = jnp.logical_and(
            jnp.broadcast_to(shard_row, (CAP, CAP)) == shard_col, lan < sub
        )
        rank_col = jnp.sum(jnp.where(same, 1.0, 0.0), axis=1, keepdims=True)
        place = shard_col * HELD + rank_col.astype(i32)
        place_v[...] = jnp.where(place == iota((CAP, LIST), 1), 1.0, 0.0).astype(bf16)

    def order_rows(i):
        y_off = (Y_OFFSETS + (0,))[i]
        q = (y + y_off) % NY
        for j, off in enumerate(X_OFFSETS):
            slot = q * NE + (me + NE - off) % NE
            arrive(got_rows.at[slot], rows_sem.at[i, j], 2)
        block = got_rows[pl.ds(q * NE, NE)].reshape(LIST, Q)
        ordered = jnp.dot(place_v[...], block, preferred_element_type=f32).astype(bf16)
        x_v[q] = ordered
        if y_off:
            send(x_v.at[q], x_got.at[y], 3, x_sem.at[y_off - 1], at_y(y_off))
        else:
            x_got[y] = ordered

    def gate_wait(sem, k, off, back):
        row = ((y + NY - off) % NY) * NZ + (z + NZ - k * back) % NZ
        arrive(gate_w.at[row], sem.at[k - 1, off], 0)
        return row

    def up_wait(sem, k, back):
        row = y * NZ + (z + NZ - k * back) % NZ
        arrive(up_w.at[row], sem.at[k - 1], 1)
        return row

    def up_across(row, slot):
        for off in Y_OFFSETS:
            send(up_w.at[row], up_w.at[row], 1, uy_sem.at[slot, off - 1], at_y(off))

    def ring(k):
        plus, minus = k < 8, k < 7
        row = up_wait(up_sem, k, 1)
        if plus:
            send(up_w.at[row], up_w.at[row], 1, up_sem.at[k], at_z(1))
        up_across(row, k)
        if plus:
            row = up_wait(um_sem, k, NZ - 1)
            if minus:
                send(up_w.at[row], up_w.at[row], 1, um_sem.at[k], at_z(NZ - 1))
            up_across(row, k + 8)
        for off in (0,) + Y_OFFSETS:
            row = gate_wait(gp_sem, k, off, 1)
            if plus:
                send(gate_w.at[row], gate_w.at[row], 0, gp_sem.at[k, off], at_z(1))
                row = gate_wait(gm_sem, k, off, NZ - 1)
            if minus:
                send(gate_w.at[row], gate_w.at[row], 0, gm_sem.at[k, off], at_z(NZ - 1))

    for load in loads:
        load.wait()
    gather(0)
    for off in Y_OFFSETS:
        row = ((y + NY - off) % NY) * NZ + z
        arrive(gate_w.at[row], gy_sem.at[off - 1], 0)
        send(gate_w.at[row], gate_w.at[row], 0, gp_sem.at[0, off], at_z(1))
        send(gate_w.at[row], gate_w.at[row], 0, gm_sem.at[0, off], at_z(NZ - 1))
    gather(1)
    ring(1)
    gather(2)
    gather(3)
    own_places()
    ring(2)
    order_rows(0)
    ring(3)
    ring(4)
    order_rows(1)
    ring(5)
    order_rows(2)
    ring(6)
    ring(7)
    ring(8)
    order_rows(3)

    @pl.loop(0, NZ)
    def _(slot):
        back = jnp.where(slot < 9, NZ - slot, slot - 8)
        for off in Y_OFFSETS:
            row = ((y + NY - off) % NY) * NZ + (z + back) % NZ
            arrive(up_w.at[row], uy_sem.at[slot, off - 1], 1)

    count = count_ref[...]

    def send_delta(m, half):
        span = pl.ds(half * HALF, HALF)
        for off in Y_OFFSETS:
            send(
                deltas.at[m * NY + y, span],
                deltas.at[m * NY + y, span],
                4,
                delta_sem.at[2 * m + half, off - 1],
                at_y(off),
            )

    for half in range(2):
        for w, columns in ((gate_w, pl.ds(0, FIRST)), (up_w, pl.ds(FIRST, BOTH - FIRST))):
            total = None
            for q in range(NY):
                part = jnp.dot(
                    x_v[q, pl.ds(half * HALF, HALF)],
                    w[pl.ds(q * NZ, NZ)].reshape(Q, w.shape[2]),
                    preferred_element_type=f32,
                )
                total = part if total is None else total + part
            act_v[:, columns] = total

        @pl.loop(0, HALF // 32)
        def _(i):
            from_act = pl.ds(pl.multiple_of(i * 32, 32), 32)
            span = pl.ds(pl.multiple_of(half * HALF + i * 32, 32), 32)
            gate_value = act_v[from_act, 0:F]
            up_value = act_v[from_act, F:BOTH]
            sigmoid = 1.0 / (1.0 + jnp.exp(-gate_value))
            activated = gate_value * sigmoid
            slope = sigmoid * (1.0 + gate_value * (1.0 - sigmoid))
            live = jnp.where(iota((32, F), 0) + (half * HALF + i * 32) < count, 1.0, 0.0)
            residual = (
                (activated * up_value - targets_v[span, :].astype(f32))
                * live
                / count.astype(f32)
            )
            deltas[y, span, :] = (residual * up_value * slope).astype(bf16)
            deltas[NY + y, span, :] = (residual * activated).astype(bf16)

        send_delta(0, half)

    for off in Y_OFFSETS:
        src = (y + NY - off) % NY
        arrive(x_got.at[src], x_sem.at[off - 1], 3)
    for s in range(NY):
        x_turned[s] = x_got[s].T

    pairs = [(a, b) for a in range(NY) for b in range(a, NY)]
    for m in range(2):
        for off in Y_OFFSETS:
            src = m * NY + (y + NY - off) % NY
            for half in range(2):
                span = pl.ds(half * HALF, HALF)
                arrive(deltas.at[src, span], delta_sem.at[2 * m + half, off - 1], 4)
        for s in range(NY):
            grads[m * NY + s] = jnp.dot(
                x_turned[s], deltas[m * NY + s], preferred_element_type=f32
            )

        def add_products(i, sums):
            span = pl.ds(pl.multiple_of(i * 8, 8), 8)
            parts = [grads[m * NY + s, span, :] for s in range(NY)]
            out = []
            for (a, b), old in zip(pairs, sums):
                product = parts[a] * parts[b]
                for c in range(F // 128):
                    old = old + product[:, c * 128 : c * 128 + 128]
                out.append(old)
            return tuple(out)

        sums = lax.fori_loop(
            0, Q // 8, add_products, tuple(jnp.zeros((8, 128), f32) for _ in pairs)
        )
        for (a, b), value in zip(pairs, sums):
            line = jnp.sum(value, axis=0, keepdims=True)
            gram_y[m * NY + y, 4 * a + b : 4 * a + b + 1, :] = line
            if a != b:
                gram_y[m * NY + y, 4 * b + a : 4 * b + a + 1, :] = line
        for off in Y_OFFSETS:
            send(
                gram_y.at[m * NY + y],
                gram_y.at[m * NY + y],
                5,
                gram_sem.at[m, off - 1],
                at_y(off),
            )
        if m == 0:
            send_delta(1, 0)
            send_delta(1, 1)

        for off in Y_OFFSETS:
            src = m * NY + (y + NY - off) % NY
            arrive(gram_y.at[src], gram_sem.at[m, off - 1], 5)
        table = gram_y[m * NY]
        for s in range(1, NY):
            table = table + gram_y[m * NY + s]
        table = jnp.broadcast_to(jnp.sum(table, axis=1, keepdims=True), (16, 128))
        scale = [lanes(c) for c in four_coefficients(table)]
        for off in Z_OFFSETS + (0,):
            to = (z + off) % NZ
            span = pl.ds(pl.multiple_of(to * ROWS, ROWS), ROWS)
            item = scale[0] * grads[m * NY, span, :]
            for s in range(1, NY):
                item = item + scale[s] * grads[m * NY + s, span, :]
            if off:
                item_out[m * NZ + to] = item.astype(bf16)
                send(
                    item_out.at[m * NZ + to],
                    item_in.at[m * NZ + z],
                    6,
                    item_sem.at[m, off - 1],
                    at_z(off),
                )
            else:
                item_in[m * NZ + z] = item.astype(bf16)

    block = NZ * ROWS
    wide_row = iota((NZ, 128), 0)
    wide_lane = iota((NZ, 128), 1)
    for m in range(2):
        for off in Z_OFFSETS:
            src = m * NZ + (z + NZ - off) % NZ
            arrive(item_in.at[src], item_sem.at[m, off - 1], 6)
        items = item_in[pl.ds(m * NZ, NZ)].reshape(block, F)
        product = lax.dot_general(
            items, items, (((1,), (1,)), ((), ())), preferred_element_type=f32
        )
        product = jnp.where(
            iota((block, block), 0) % ROWS == iota((block, block), 1) % ROWS, product, 0.0
        )
        product = jnp.sum(product.reshape(NZ, ROWS, block), axis=1)
        fold = jnp.where(
            iota((block, 128), 0) // ROWS == iota((block, 128), 1) % NZ, 1.0, 0.0
        )
        gram = jnp.dot(
            product, fold, precision=lax.Precision.HIGHEST, preferred_element_type=f32
        )
        packed = jnp.where(wide_row % 8 == wide_lane // NZ, gram, 0.0)
        tab_y[y, pl.ds(2 * m, 2), :] = jnp.sum(packed.reshape(2, 8, 128), axis=1)
    for off in Y_OFFSETS:
        send(tab_y.at[y], tab_y.at[y], 7, ty_sem.at[off - 1], at_y(off))
    for off in Y_OFFSETS:
        src = (y + NY - off) % NY
        arrive(tab_y.at[src], ty_sem.at[off - 1], 7)
    tab_z[z] = jnp.sum(tab_y[...], axis=0)
    for off in Z_OFFSETS:
        send(tab_z.at[z], tab_z.at[z], 8, tz_sem.at[off - 1], at_z(off))
    for off in Z_OFFSETS:
        src = (z + NZ - off) % NZ
        arrive(tab_z.at[src], tz_sem.at[off - 1], 8)
    table = jnp.sum(tab_z[...], axis=0)
    for m in range(2):
        gram = jnp.concatenate(
            [
                jnp.broadcast_to(table[j : j + 1, :], (8, 128))
                for j in (2 * m, 2 * m + 1)
            ],
            axis=0,
        )
        gram = jnp.where(wide_row % 8 == wide_lane // NZ, gram, 0.0)
        for turn in (16, 32, 64):
            gram = gram + pltpu.roll(gram, turn, 1)
        scale = jnp.broadcast_to(ring_coefficients(gram), (NZ, 128))
        total = None
        for s in range(NZ):
            term = lanes(scale[s : s + 1, :]) * item_in[m * NZ + s].astype(f32)
            total = term if total is None else total + term
        out_ref[m] = total

    arrive(gate_w.at[pl.ds(0, 63)], send_sem.at[0], 0)
    arrive(up_w.at[pl.ds(0, 63)], send_sem.at[1], 1)
    arrive(sent_rows.at[pl.ds(0, 28)], send_sem.at[2], 2)
    arrive(x_v.at[pl.ds(0, 3)], send_sem.at[3], 3)
    arrive(deltas.at[pl.ds(0, 6)], send_sem.at[4], 4)
    arrive(gram_y.at[pl.ds(0, 6)], send_sem.at[5], 5)
    arrive(item_out.at[pl.ds(0, 30)], send_sem.at[6], 6)
    arrive(tab_y.at[pl.ds(0, 3)], send_sem.at[7], 7)
    arrive(tab_z.at[pl.ds(0, 15)], send_sem.at[8], 8)


def combined_gradient(pool, row_index, counts, targets, weights):
    vmem = pl.BlockSpec(memory_space=pltpu.VMEM)
    anywhere = pl.BlockSpec(memory_space=pl.ANY)
    dma = pltpu.SemaphoreType.DMA
    return pl.pallas_call(
        step_kernel,
        out_shape=jax.ShapeDtypeStruct((2, ROWS, F), f32),
        in_specs=[vmem, vmem, anywhere, anywhere, vmem],
        out_specs=vmem,
        scratch_shapes=[
            pltpu.VMEM((NY, SHARD, Q), bf16),
            pltpu.VMEM((CAP, F), bf16),
            pltpu.VMEM((NE, CAP), f32),
            pltpu.VMEM((LIST, SHARD), bf16),
            pltpu.VMEM((CAP, LIST), bf16),
            pltpu.VMEM((NY * NE, HELD, Q), bf16),
            pltpu.VMEM((NY * NE, HELD, Q), bf16),
            pltpu.VMEM((NY, CAP, Q), bf16),
            pltpu.VMEM((NY, CAP, Q), bf16),
            pltpu.VMEM((NY, Q, CAP), bf16),
            pltpu.VMEM((NR, ROWS, FIRST), bf16),
            pltpu.VMEM((NR, ROWS, BOTH - FIRST), bf16),
            pltpu.VMEM((HALF, BOTH), f32),
            pltpu.VMEM((2 * NY, CAP, F), bf16),
            pltpu.VMEM((2 * NY, Q, F), f32),
            pltpu.VMEM((2 * NY, 16, 128), f32),
            pltpu.VMEM((2 * NZ, ROWS, F), bf16),
            pltpu.VMEM((2 * NZ, ROWS, F), bf16),
            pltpu.VMEM((NY, 4, 128), f32),
            pltpu.VMEM((NZ, 4, 128), f32),
            dma((NY + 1,)),
            dma((9,)),
            dma((NY, NE - 1)),
            dma((NY - 1,)),
            dma((8, NY)),
            dma((7, NY)),
            dma((8,)),
            dma((7,)),
            dma((NZ, NY - 1)),
            dma((NY - 1,)),
            dma((4, NY - 1)),
            dma((2, NY - 1)),
            dma((2, NZ - 1)),
            dma((NY - 1,)),
            dma((NZ - 1,)),
        ],
        compiler_params=pltpu.CompilerParams(
            collective_id=0, has_side_effects=True, vmem_limit_bytes=56 * 1024 * 1024
        ),
    )(row_index, counts, pool, targets, weights)


def shards(pool, row_index, counts, targets, weights, first_moment, second_moment):
    combined = combined_gradient(pool, row_index, counts, targets, weights)
    new_weight, moment_one, moment_two = adam_update(
        combined, weights[0], first_moment[0], second_moment[0]
    )
    return (new_weight[None], moment_one[None], moment_two[None])


def solution(mesh):
    in_specs = (
        P("replica", "expert", None),
        P(None, "replica", None),
        P("expert", "replica"),
        P("expert", "replica", None, None),
        P("expert", None, "replica", None),
        P("expert", None, "replica", None),
        P("expert", None, "replica", None),
    )
    out_specs = (P("expert", None, "replica", None),) * 3
    return jax.shard_map(
        shards, mesh=mesh, in_specs=in_specs, out_specs=out_specs, check_vma=False
    )
```

```python
import functools

import jax
import jax.numpy as jnp
from jax import lax
from jax.experimental import pallas as pl
from jax.experimental.pallas import tpu as pltpu
from jax.sharding import PartitionSpec as P

STEP = 3
MESH = pl.DeviceIdType.MESH
NE, NY, NZ = 8, 4, 16
NR = NY * NZ
CAP = 256
HELD = 48
D = 2048
F = 384
SHARD = 512
Q = D // NY
ROWS = D // NR
LIST = NE * HELD
HALF = CAP // 2
BOTH = 2 * F
FIRST = 512

beta_first = 0.9
beta_second = 0.999
learning_rate = 0.02
decay_rate = 0.1
adam_epsilon = 1e-08
adasum_epsilon = 1e-12

f32 = jnp.float32
bf16 = jnp.bfloat16
i32 = jnp.int32

X_OFFSETS = (4, 3, 5, 2, 6, 7, 1)
Y_OFFSETS = (2, 1, 3)
Z_OFFSETS = (8, 7, 9, 6, 10, 5, 11, 4, 12, 3, 13, 2, 14, 1, 15)


def iota(shape, dim):
    return lax.broadcasted_iota(i32, shape, dim)


def adam_update(gradient, weight, moment_one, moment_two):
    moment_one = beta_first * moment_one + (1.0 - beta_first) * gradient
    moment_two = beta_second * moment_two + (1.0 - beta_second) * gradient * gradient
    first_hat = moment_one / (1.0 - beta_first**STEP)
    second_hat = moment_two / (1.0 - beta_second**STEP)
    weight = weight - learning_rate * (
        first_hat / (jnp.sqrt(second_hat) + adam_epsilon) + decay_rate * weight
    )
    return (weight, moment_one, moment_two)


def pair_weights(inner, first_square, second_square):
    first = 1.0 - inner / (2.0 * first_square + adasum_epsilon)
    second = 1.0 - inner / (2.0 * second_square + adasum_epsilon)
    return first, second


def four_coefficients(rows):
    g = lambda a, b: rows[4 * a + b : 4 * a + b + 1, :]
    w0, w2 = pair_weights(g(0, 2), g(0, 0), g(2, 2))
    w1, w3 = pair_weights(g(1, 3), g(1, 1), g(3, 3))
    qa = w0 * w0 * g(0, 0) + 2.0 * w0 * w2 * g(0, 2) + w2 * w2 * g(2, 2)
    qb = w1 * w1 * g(1, 1) + 2.0 * w1 * w3 * g(1, 3) + w3 * w3 * g(3, 3)
    qa = jnp.maximum(qa, 0.0)
    qb = jnp.maximum(qb, 0.0)
    pab = w0 * (w1 * g(0, 1) + w3 * g(0, 3)) + w2 * (w1 * g(2, 1) + w3 * g(2, 3))
    va, vb = pair_weights(pab, qa, qb)
    return (va * w0, vb * w1, va * w2, vb * w3)


def ring_coefficients(gram):
    row = iota((NZ, 128), 0)
    lane = iota((NZ, 128), 1)
    coefficient = jnp.ones((NZ, 1), f32)
    for half in (8, 4, 2, 1):
        zero = jnp.zeros_like(gram)
        p_col = jnp.sum(jnp.where(lane == (row + half) % NZ, gram, zero), axis=1, keepdims=True)
        q_col = jnp.sum(jnp.where(lane == row, gram, zero), axis=1, keepdims=True)
        p_row = jnp.sum(
            jnp.where(row == (lane + half) % NZ, gram, zero), axis=0, keepdims=True
        )
        q_row = jnp.sum(jnp.where(row == lane % NZ, gram, zero), axis=0, keepdims=True)
        w_col = 1.0 - p_col / (2.0 * jnp.maximum(q_col, 0.0) + adasum_epsilon)
        w_row = 1.0 - p_row / (2.0 * jnp.maximum(q_row, 0.0) + adasum_epsilon)
        scaled = w_col * gram * w_row
        folded = scaled + pltpu.roll(scaled, half, 1)
        gram = folded + pltpu.roll(folded, half, 0)
        coefficient = coefficient * w_col
    return coefficient


def lanes(row):
    return jnp.concatenate([row] * (F // 128), axis=1)


def step_kernel(
    rows_ref,
    count_ref,
    pool_hbm,
    targets_hbm,
    weights_ref,
    out_ref,
    pool_v,
    targets_v,
    held_v,
    pick_v,
    place_v,
    sent_rows,
    got_rows,
    x_v,
    x_got,
    x_turned,
    gate_w,
    up_w,
    act_v,
    deltas,
    grads,
    gram_y,
    item_out,
    item_in,
    tab_y,
    tab_z,
    load_sem,
    send_sem,
    rows_sem,
    gy_sem,
    gp_sem,
    gm_sem,
    up_sem,
    um_sem,
    uy_sem,
    x_sem,
    delta_sem,
    gram_sem,
    item_sem,
    ty_sem,
    tz_sem,
):
    me = lax.axis_index("expert")
    rep = lax.axis_index("replica")
    y = rep // NZ
    z = rep % NZ

    def at_e(off):
        return ((me + off) % NE, rep)

    def at_y(off):
        return (me, ((y + off) % NY) * NZ + z)

    def at_z(off):
        return (me, y * NZ + (z + off) % NZ)

    def send(src, dst, group, recv, device):
        pltpu.make_async_remote_copy(
            src_ref=src,
            dst_ref=dst,
            send_sem=send_sem.at[group],
            recv_sem=recv,
            device_id=device,
            device_id_type=MESH,
        ).start()

    def arrive(ref, sem, group):
        pltpu.make_async_copy(ref, ref, sem).wait()

    barrier = pltpu.get_barrier_semaphore()
    peers = [at_e(o) for o in X_OFFSETS] + [at_y(o) for o in Y_OFFSETS] + [at_z(1), at_z(NZ - 1)]
    for device in peers:
        pl.semaphore_signal(barrier, inc=1, device_id=device, device_id_type=MESH)

    loads = [
        pltpu.make_async_copy(
            pool_hbm.at[0, :, pl.ds(q * Q, Q)], pool_v.at[q], load_sem.at[q]
        )
        for q in range(NY)
    ]
    loads.append(pltpu.make_async_copy(targets_hbm.at[0, 0], targets_v, load_sem.at[NY]))
    for load in loads:
        load.start()

    gate_w[rep, :, pl.ds(0, F)] = weights_ref[0, 0].astype(bf16)
    gate_w[rep, :, pl.ds(F, FIRST - F)] = weights_ref[0, 1, :, pl.ds(0, FIRST - F)].astype(bf16)
    up_w[rep] = weights_ref[0, 1, :, pl.ds(FIRST - F, BOTH - FIRST)].astype(bf16)

    for e in range(NE):
        listed = rows_ref[e]
        held_v[e : e + 1, :] = jnp.where(listed // SHARD == me, 1.0, 0.0)
    before = jnp.where(iota((CAP, CAP), 0) < iota((CAP, CAP), 1), 1.0, 0.0).astype(bf16)
    held = held_v[...]
    rank = jnp.dot(held.astype(bf16), before, preferred_element_type=f32)
    held_v[...] = jnp.where(held > 0.5, rank, -1.0)
    for e in range(NE):
        key = jnp.broadcast_to(held_v[e : e + 1, :], (HELD, CAP))
        local = jnp.broadcast_to((rows_ref[e] - me * SHARD + 1).astype(f32), (HELD, CAP))
        match = key == iota((HELD, CAP), 0).astype(f32)
        index = jnp.sum(jnp.where(match, local, 0.0), axis=1, keepdims=True) - 1.0
        pick_v[pl.ds(e * HELD, HELD), :] = jnp.where(
            index == iota((HELD, SHARD), 1).astype(f32), 1.0, 0.0
        ).astype(bf16)

    pl.semaphore_wait(barrier, len(peers))

    for off in Y_OFFSETS:
        send(gate_w.at[rep], gate_w.at[rep], 0, gy_sem.at[off - 1], at_y(off))
    send(up_w.at[rep], up_w.at[rep], 1, up_sem.at[0], at_z(1))
    send(up_w.at[rep], up_w.at[rep], 1, um_sem.at[0], at_z(NZ - 1))
    send(gate_w.at[rep], gate_w.at[rep], 0, gp_sem.at[0, 0], at_z(1))
    send(gate_w.at[rep], gate_w.at[rep], 0, gm_sem.at[0, 0], at_z(NZ - 1))
    for off in Y_OFFSETS:
        send(up_w.at[rep], up_w.at[rep], 1, uy_sem.at[0, off - 1], at_y(off))

    def gather(i):
        q = (y + (Y_OFFSETS + (0,))[i]) % NY
        found = jnp.dot(pick_v[...], pool_v[q], preferred_element_type=f32).astype(bf16)
        sent_rows[pl.ds(q * NE, NE)] = found.reshape(NE, HELD, Q)
        for j, off in enumerate(X_OFFSETS):
            send(
                sent_rows.at[q * NE + (me + off) % NE],
                got_rows.at[q * NE + me],
                2,
                rows_sem.at[i, j],
                at_e(off),
            )
        got_rows[q * NE + me] = sent_rows[q * NE + me]

    def own_places():
        own_row = rows_ref[me].astype(f32)
        square = jnp.broadcast_to(own_row, (CAP, CAP))
        sub = iota((CAP, CAP), 0)
        lan = iota((CAP, CAP), 1)
        own_col = jnp.sum(jnp.where(sub == lan, square, 0.0), axis=1, keepdims=True)
        shard_row = rows_ref[me] // SHARD
        shard_col = own_col.astype(i32) // SHARD
        same = jnp.logical_and(
            jnp.broadcast_to(shard_row, (CAP, CAP)) == shard_col, lan < sub
        )
        rank_col = jnp.sum(jnp.where(same, 1.0, 0.0), axis=1, keepdims=True)
        place = shard_col * HELD + rank_col.astype(i32)
        place_v[...] = jnp.where(place == iota((CAP, LIST), 1), 1.0, 0.0).astype(bf16)

    def order_rows(i):
        y_off = (Y_OFFSETS + (0,))[i]
        q = (y + y_off) % NY
        for j, off in enumerate(X_OFFSETS):
            slot = q * NE + (me + NE - off) % NE
            arrive(got_rows.at[slot], rows_sem.at[i, j], 2)
        block = got_rows[pl.ds(q * NE, NE)].reshape(LIST, Q)
        ordered = jnp.dot(place_v[...], block, preferred_element_type=f32).astype(bf16)
        x_v[q] = ordered
        if y_off:
            send(x_v.at[q], x_got.at[y], 3, x_sem.at[y_off - 1], at_y(y_off))
        else:
            x_got[y] = ordered

    def gate_wait(sem, k, off, back):
        row = ((y + NY - off) % NY) * NZ + (z + NZ - k * back) % NZ
        arrive(gate_w.at[row], sem.at[k - 1, off], 0)
        return row

    def up_wait(sem, k, back):
        row = y * NZ + (z + NZ - k * back) % NZ
        arrive(up_w.at[row], sem.at[k - 1], 1)
        return row

    def up_across(row, slot):
        for off in Y_OFFSETS:
            send(up_w.at[row], up_w.at[row], 1, uy_sem.at[slot, off - 1], at_y(off))

    def ring(k):
        plus, minus = k < 8, k < 7
        row = up_wait(up_sem, k, 1)
        if plus:
            send(up_w.at[row], up_w.at[row], 1, up_sem.at[k], at_z(1))
        up_across(row, k)
        if plus:
            row = up_wait(um_sem, k, NZ - 1)
            if minus:
                send(up_w.at[row], up_w.at[row], 1, um_sem.at[k], at_z(NZ - 1))
            up_across(row, k + 8)
        for off in (0,) + Y_OFFSETS:
            row = gate_wait(gp_sem, k, off, 1)
            if plus:
                send(gate_w.at[row], gate_w.at[row], 0, gp_sem.at[k, off], at_z(1))
                row = gate_wait(gm_sem, k, off, NZ - 1)
            if minus:
                send(gate_w.at[row], gate_w.at[row], 0, gm_sem.at[k, off], at_z(NZ - 1))

    for load in loads:
        load.wait()
    for i in range(NY):
        gather(i)
    own_places()
    for off in Y_OFFSETS:
        row = ((y + NY - off) % NY) * NZ + z
        arrive(gate_w.at[row], gy_sem.at[off - 1], 0)
        send(gate_w.at[row], gate_w.at[row], 0, gp_sem.at[0, off], at_z(1))
        send(gate_w.at[row], gate_w.at[row], 0, gm_sem.at[0, off], at_z(NZ - 1))
    ring(1)
    ring(2)
    order_rows(0)
    ring(3)
    order_rows(1)
    ring(4)
    ring(5)
    order_rows(2)
    ring(6)
    ring(7)
    ring(8)
    order_rows(3)

    def multiply(w, columns, slots):
        total = None
        for q in range(NY):
            part = jnp.dot(
                x_v[q, slots], w[pl.ds(q * NZ, NZ)].reshape(Q, w.shape[2]), preferred_element_type=f32
            )
            total = part if total is None else total + part
        act_v[slots, columns] = total

    multiply(gate_w, pl.ds(0, FIRST), pl.ds(0, CAP))

    @pl.loop(0, NZ)
    def _(slot):
        back = jnp.where(slot < 9, NZ - slot, slot - 8)
        for off in Y_OFFSETS:
            row = ((y + NY - off) % NY) * NZ + (z + back) % NZ
            arrive(up_w.at[row], uy_sem.at[slot, off - 1], 1)

    count = count_ref[...]

    def send_delta(m, half):
        span = pl.ds(half * HALF, HALF)
        for off in Y_OFFSETS:
            send(
                deltas.at[m * NY + y, span],
                deltas.at[m * NY + y, span],
                4,
                delta_sem.at[2 * m + half, off - 1],
                at_y(off),
            )

    for half in range(2):
        multiply(up_w, pl.ds(FIRST, BOTH - FIRST), pl.ds(half * HALF, HALF))

        @pl.loop(0, HALF // 32)
        def _(i):
            span = pl.ds(pl.multiple_of(half * HALF + i * 32, 32), 32)
            gate_value = act_v[span, 0:F]
            up_value = act_v[span, F:BOTH]
            sigmoid = 1.0 / (1.0 + jnp.exp(-gate_value))
            activated = gate_value * sigmoid
            slope = sigmoid * (1.0 + gate_value * (1.0 - sigmoid))
            live = jnp.where(iota((32, F), 0) + (half * HALF + i * 32) < count, 1.0, 0.0)
            residual = (
                (activated * up_value - targets_v[span, :].astype(f32))
                * live
                / count.astype(f32)
            )
            deltas[y, span, :] = (residual * up_value * slope).astype(bf16)
            deltas[NY + y, span, :] = (residual * activated).astype(bf16)

        send_delta(0, half)

    for off in Y_OFFSETS:
        src = (y + NY - off) % NY
        arrive(x_got.at[src], x_sem.at[off - 1], 3)
    for s in range(NY):
        x_turned[s] = x_got[s].T

    pairs = [(a, b) for a in range(NY) for b in range(a, NY)]
    for m in range(2):
        for off in Y_OFFSETS:
            src = m * NY + (y + NY - off) % NY
            for half in range(2):
                span = pl.ds(half * HALF, HALF)
                arrive(deltas.at[src, span], delta_sem.at[2 * m + half, off - 1], 4)
        for s in range(NY):
            grads[m * NY + s] = jnp.dot(
                x_turned[s], deltas[m * NY + s], preferred_element_type=f32
            )

        def add_products(i, sums):
            span = pl.ds(pl.multiple_of(i * 8, 8), 8)
            parts = [grads[m * NY + s, span, :] for s in range(NY)]
            out = []
            for (a, b), old in zip(pairs, sums):
                product = parts[a] * parts[b]
                for c in range(F // 128):
                    old = old + product[:, c * 128 : c * 128 + 128]
                out.append(old)
            return tuple(out)

        sums = lax.fori_loop(
            0, Q // 8, add_products, tuple(jnp.zeros((8, 128), f32) for _ in pairs)
        )
        for (a, b), value in zip(pairs, sums):
            line = jnp.sum(value, axis=0, keepdims=True)
            gram_y[m * NY + y, 4 * a + b : 4 * a + b + 1, :] = line
            if a != b:
                gram_y[m * NY + y, 4 * b + a : 4 * b + a + 1, :] = line
        for off in Y_OFFSETS:
            send(
                gram_y.at[m * NY + y],
                gram_y.at[m * NY + y],
                5,
                gram_sem.at[m, off - 1],
                at_y(off),
            )
        if m == 0:
            send_delta(1, 0)
            send_delta(1, 1)

        for off in Y_OFFSETS:
            src = m * NY + (y + NY - off) % NY
            arrive(gram_y.at[src], gram_sem.at[m, off - 1], 5)
        table = gram_y[m * NY]
        for s in range(1, NY):
            table = table + gram_y[m * NY + s]
        table = jnp.broadcast_to(jnp.sum(table, axis=1, keepdims=True), (16, 128))
        scale = [lanes(c) for c in four_coefficients(table)]
        for off in Z_OFFSETS + (0,):
            to = (z + off) % NZ
            span = pl.ds(pl.multiple_of(to * ROWS, ROWS), ROWS)
            item = scale[0] * grads[m * NY, span, :]
            for s in range(1, NY):
                item = item + scale[s] * grads[m * NY + s, span, :]
            if off:
                item_out[m * NZ + to] = item.astype(bf16)
                send(
                    item_out.at[m * NZ + to],
                    item_in.at[m * NZ + z],
                    6,
                    item_sem.at[m, off - 1],
                    at_z(off),
                )
            else:
                item_in[m * NZ + z] = item.astype(bf16)

    block = NZ * ROWS
    wide_row = iota((NZ, 128), 0)
    wide_lane = iota((NZ, 128), 1)
    for m in range(2):
        for off in Z_OFFSETS:
            src = m * NZ + (z + NZ - off) % NZ
            arrive(item_in.at[src], item_sem.at[m, off - 1], 6)
        items = item_in[pl.ds(m * NZ, NZ)].reshape(block, F)
        product = lax.dot_general(
            items, items, (((1,), (1,)), ((), ())), preferred_element_type=f32
        )
        product = jnp.where(
            iota((block, block), 0) % ROWS == iota((block, block), 1) % ROWS, product, 0.0
        )
        product = jnp.sum(product.reshape(NZ, ROWS, block), axis=1)
        fold = jnp.where(
            iota((block, 128), 0) // ROWS == iota((block, 128), 1) % NZ, 1.0, 0.0
        )
        gram = jnp.dot(
            product, fold, precision=lax.Precision.HIGHEST, preferred_element_type=f32
        )
        packed = jnp.where(wide_row % 8 == wide_lane // NZ, gram, 0.0)
        tab_y[y, pl.ds(2 * m, 2), :] = jnp.sum(packed.reshape(2, 8, 128), axis=1)
    for off in Y_OFFSETS:
        send(tab_y.at[y], tab_y.at[y], 7, ty_sem.at[off - 1], at_y(off))
    for off in Y_OFFSETS:
        src = (y + NY - off) % NY
        arrive(tab_y.at[src], ty_sem.at[off - 1], 7)
    tab_z[z] = jnp.sum(tab_y[...], axis=0)
    for off in Z_OFFSETS:
        send(tab_z.at[z], tab_z.at[z], 8, tz_sem.at[off - 1], at_z(off))
    for off in Z_OFFSETS:
        src = (z + NZ - off) % NZ
        arrive(tab_z.at[src], tz_sem.at[off - 1], 8)
    table = jnp.sum(tab_z[...], axis=0)
    for m in range(2):
        gram = jnp.concatenate(
            [
                jnp.broadcast_to(table[j : j + 1, :], (8, 128))
                for j in (2 * m, 2 * m + 1)
            ],
            axis=0,
        )
        gram = jnp.where(wide_row % 8 == wide_lane // NZ, gram, 0.0)
        for turn in (16, 32, 64):
            gram = gram + pltpu.roll(gram, turn, 1)
        scale = jnp.broadcast_to(ring_coefficients(gram), (NZ, 128))
        total = None
        for s in range(NZ):
            term = lanes(scale[s : s + 1, :]) * item_in[m * NZ + s].astype(f32)
            total = term if total is None else total + term
        out_ref[m] = total

    arrive(gate_w.at[pl.ds(0, 63)], send_sem.at[0], 0)
    arrive(up_w.at[pl.ds(0, 63)], send_sem.at[1], 1)
    arrive(sent_rows.at[pl.ds(0, 28)], send_sem.at[2], 2)
    arrive(x_v.at[pl.ds(0, 3)], send_sem.at[3], 3)
    arrive(deltas.at[pl.ds(0, 6)], send_sem.at[4], 4)
    arrive(gram_y.at[pl.ds(0, 6)], send_sem.at[5], 5)
    arrive(item_out.at[pl.ds(0, 30)], send_sem.at[6], 6)
    arrive(tab_y.at[pl.ds(0, 3)], send_sem.at[7], 7)
    arrive(tab_z.at[pl.ds(0, 15)], send_sem.at[8], 8)


def combined_gradient(pool, row_index, counts, targets, weights):
    vmem = pl.BlockSpec(memory_space=pltpu.VMEM)
    anywhere = pl.BlockSpec(memory_space=pl.ANY)
    dma = pltpu.SemaphoreType.DMA
    return pl.pallas_call(
        step_kernel,
        out_shape=jax.ShapeDtypeStruct((2, ROWS, F), f32),
        in_specs=[vmem, vmem, anywhere, anywhere, vmem],
        out_specs=vmem,
        scratch_shapes=[
            pltpu.VMEM((NY, SHARD, Q), bf16),
            pltpu.VMEM((CAP, F), bf16),
            pltpu.VMEM((NE, CAP), f32),
            pltpu.VMEM((LIST, SHARD), bf16),
            pltpu.VMEM((CAP, LIST), bf16),
            pltpu.VMEM((NY * NE, HELD, Q), bf16),
            pltpu.VMEM((NY * NE, HELD, Q), bf16),
            pltpu.VMEM((NY, CAP, Q), bf16),
            pltpu.VMEM((NY, CAP, Q), bf16),
            pltpu.VMEM((NY, Q, CAP), bf16),
            pltpu.VMEM((NR, ROWS, FIRST), bf16),
            pltpu.VMEM((NR, ROWS, BOTH - FIRST), bf16),
            pltpu.VMEM((CAP, BOTH), f32),
            pltpu.VMEM((2 * NY, CAP, F), bf16),
            pltpu.VMEM((2 * NY, Q, F), f32),
            pltpu.VMEM((2 * NY, 16, 128), f32),
            pltpu.VMEM((2 * NZ, ROWS, F), bf16),
            pltpu.VMEM((2 * NZ, ROWS, F), bf16),
            pltpu.VMEM((NY, 4, 128), f32),
            pltpu.VMEM((NZ, 4, 128), f32),
            dma((NY + 1,)),
            dma((9,)),
            dma((NY, NE - 1)),
            dma((NY - 1,)),
            dma((8, NY)),
            dma((7, NY)),
            dma((8,)),
            dma((7,)),
            dma((NZ, NY - 1)),
            dma((NY - 1,)),
            dma((4, NY - 1)),
            dma((2, NY - 1)),
            dma((2, NZ - 1)),
            dma((NY - 1,)),
            dma((NZ - 1,)),
        ],
        compiler_params=pltpu.CompilerParams(
            collective_id=0, has_side_effects=True, vmem_limit_bytes=56 * 1024 * 1024
        ),
    )(row_index, counts, pool, targets, weights)


def shards(pool, row_index, counts, targets, weights, first_moment, second_moment):
    combined = combined_gradient(pool, row_index, counts, targets, weights)
    new_weight, moment_one, moment_two = adam_update(
        combined, weights[0], first_moment[0], second_moment[0]
    )
    return (new_weight[None], moment_one[None], moment_two[None])


def solution(mesh):
    in_specs = (
        P("replica", "expert", None),
        P(None, "replica", None),
        P("expert", "replica"),
        P("expert", "replica", None, None),
        P("expert", None, "replica", None),
        P("expert", None, "replica", None),
        P("expert", None, "replica", None),
    )
    out_specs = (P("expert", None, "replica", None),) * 3
    return jax.shard_map(
        shards, mesh=mesh, in_specs=in_specs, out_specs=out_specs, check_vma=False
    )
```
